32 devices in a mesh: row: 2 (over x), col: 16 (over z, y, core).
Axes of the slice: x: 2, y: 2, z: 4, core: 2. Of those that a mesh axis runs over, the one named last changes fastest.
Arguments:
- features: bfloat16 [8192, 256], P(('row', 'col')), may hold values from -6 to 6
- weight: bfloat16 [256, 128], replicated, may hold values from -0.375 to 0.375
- tiles: bfloat16 [2, 16, 320, 128, 128], P('row', 'col'), may hold values from -0.0625 to 0.0625
- slot_tile_row: int32 [2, 16, 320], P('row', 'col'), may hold values from 0 to 3
- tile_cols: int32 [2, 16, 320], P('row', 'col'), may hold values from 0 to 31
- live_tiles: int32 [2, 16], P('row', 'col'), may hold values from 40 to 320, as said below
- cotangent: bfloat16 [8192, 128], P(('row', 'col')), may hold values from -6 to 6
Outputs:
- logits: bfloat16 [8192, 128], P(('row', 'col'))
- grad_features: bfloat16 [8192, 256], P(('row', 'col'))
- grad_weight: float32 [256, 128], replicated
The draws below stay inside these ranges and needn't reach their ends.
Inputs may be any that keep to these rules, and one draw needn't show every extreme that they name: Slots of a block from live_tiles on are padding and not part of the adjacency; in every draw some block has all 320 slots live.
All inputs are finite; a program needn't handle non-finite values.
Results may differ from the reference program's by a relative error of at most 0.005.
Values may be sent and summed in bfloat16 or wider, within the bound.
A program may use at most 128 MiB of HBM per device.

```python
import math
import jax
import jax.numpy as jnp
from jax import lax

F = 256
FO = 128
TILE = 128
CH = 256
NT = 320
NODES = 8192
ROW_TILES = 4
COL_TILES = 32
N_ROW = 2
N_COL = 16


def draw_live_tiles(key, part):
    key_base, key_heavy, key_forced = jax.random.split(key, 3)
    grid_shape = (N_ROW, N_COL)
    base_count = jax.random.randint(key_base, grid_shape, NT // 8, NT // 2 + 1)
    heavy_rows = jax.random.randint(key_heavy, grid_shape, 0, 4) == 0
    counts = jnp.where(heavy_rows, NT, base_count).reshape(-1)
    forced_index = jax.random.randint(key_forced, (), 0, N_ROW * N_COL)
    counts = jnp.where(jnp.arange(N_ROW * N_COL) == forced_index, NT, counts)
    return counts.reshape(grid_shape).astype(jnp.int32)


def touch_ends(result, rng, smallest, high):
    extent = result.shape
    place = [jax.random.randint(jax.random.fold_in(rng, axis), (), 0, extent[axis]) for axis in range(len(extent))]
    result = result.at[tuple(place)].set(smallest)
    longest = extent.index(max(extent))
    place[longest] = (place[longest] + 1) % extent[longest]
    return result.at[tuple(place)].set(high)


def level_of(own_key, shape, shards, smallest, high):
    gain = 1.0
    for axis_at, shards_of in shards:
        steps = jax.random.uniform(jax.random.fold_in(jax.random.fold_in(own_key, 6), axis_at), (shards_of,), jnp.float32, smallest / len(shards), high / len(shards))
        gain = gain * jnp.repeat(jnp.exp(steps), shape[axis_at] // shards_of).reshape((-1,) + (1,) * (len(shape) - 1 - axis_at))
    return gain


def gaussian(stream_key, extent, spread, most, cuts=(), kind=jnp.bfloat16):
    entries = spread * jax.random.normal(stream_key, extent, jnp.float32)
    if cuts:
        entries = entries * level_of(stream_key, extent, cuts, -0.22, 0.18)
    return jnp.clip(entries, -most, most).astype(kind)


def setup_inputs(seed: int = 0) -> dict:
    keys = jax.random.split(jax.random.key(seed), 8)
    return {
        "features": gaussian(keys[0], (NODES, F), 1.0, 6.0, ((0, 32),)),
        "weight": gaussian(keys[1], (F, FO), F ** -0.5, 0.375),
        "tiles": gaussian(keys[2], (N_ROW, N_COL, NT, TILE, TILE), (NT * TILE * TILE // (2 * CH)) ** -0.5, 0.0625, ((0, 2), (1, 16))),
        "slot_tile_row": touch_ends(jax.random.randint(keys[3], (N_ROW, N_COL, NT), 0, ROW_TILES), jax.random.fold_in(keys[3], 1), 0, ROW_TILES - 1).astype(jnp.int32),
        "tile_cols": touch_ends(jax.random.randint(keys[4], (N_ROW, N_COL, NT), 0, COL_TILES), jax.random.fold_in(keys[4], 1), 0, COL_TILES - 1).astype(jnp.int32),
        "live_tiles": draw_live_tiles(jax.random.fold_in(keys[7], 71), 0),
        "cotangent": gaussian(keys[6], (NODES, FO), 1.0, 6.0, ((0, 32),)),
    }


def device_products(tile_block, row_slots, col_slots, live_count, projected_group, cot_group):
    tiles_wide = tile_block.astype(jnp.float32)
    live_mask = jnp.arange(NT, dtype=jnp.int32) < live_count
    inputs = projected_group.astype(jnp.float32).reshape(COL_TILES, TILE, FO)[col_slots]
    products = jnp.einsum('tab,tbf->taf', tiles_wide, inputs, precision=lax.Precision.HIGHEST)
    row_onehot = ((row_slots[None, :] == jnp.arange(ROW_TILES, dtype=jnp.int32)[:, None]) & live_mask[None, :]).astype(jnp.float32)
    forward = jnp.einsum('rt,taf->raf', row_onehot, products, precision=lax.Precision.HIGHEST)
    cot_tiles = cot_group.astype(jnp.float32).reshape(ROW_TILES, TILE, FO)[row_slots]
    backward_partials = jnp.einsum('tab,taf->tbf', tiles_wide, cot_tiles, precision=lax.Precision.HIGHEST)
    column_indicator = ((col_slots[None, :] == jnp.arange(COL_TILES, dtype=jnp.int32)[:, None]) & live_mask[None, :]).astype(jnp.float32)
    backward_layer_pass = jnp.einsum('io,owe->iwe', column_indicator, backward_partials, precision=lax.Precision.HIGHEST)
    return (forward.reshape(ROW_TILES * TILE, FO), backward_layer_pass.reshape(COL_TILES * TILE, FO))

def reference(features, weight, tiles, slot_tile_row, tile_cols, live_tiles, cotangent):
    projected = jnp.dot(features, weight, preferred_element_type=jnp.float32).astype(jnp.bfloat16)
    proj_groups = projected.reshape(N_ROW, N_COL * CH, FO)
    cot_stretches = cotangent.reshape(N_ROW, N_COL, CH, FO)
    device_total = N_ROW * N_COL

    def visit(carry, inputs):
        logit_sums, back_sums = carry
        position, tile_block, row_slots, col_slots, live_count = inputs
        group_index = position // N_COL
        column_index = position % N_COL
        projected_group = proj_groups[group_index]
        cot_group = cot_stretches[:, column_index].reshape(N_ROW * CH, FO)
        forward, backward_layer_pass = device_products(tile_block, row_slots, col_slots, live_count, projected_group, cot_group)
        logit_sums = logit_sums.at[:, column_index].add(forward.reshape(N_ROW, CH, FO))
        back_sums = back_sums.at[group_index].add(backward_layer_pass)
        return ((logit_sums, back_sums), None)
    start_sums = (jnp.zeros((N_ROW, N_COL, CH, FO), jnp.float32), jnp.zeros((N_ROW, N_COL * CH, FO), jnp.float32))
    scanned = (jnp.arange(device_total, dtype=jnp.int32), tiles.reshape(device_total, NT, TILE, TILE), slot_tile_row.reshape(device_total, NT), tile_cols.reshape(device_total, NT), live_tiles.reshape(device_total))
    (logit_sums, back_sums), unused = lax.scan(visit, start_sums, scanned)
    logits = logit_sums.reshape(NODES, FO).astype(jnp.bfloat16)
    back_rounded = back_sums.reshape(NODES, FO).astype(jnp.bfloat16)
    grad_features = jnp.dot(back_rounded, weight.T, preferred_element_type=jnp.float32).astype(jnp.bfloat16)
    grad_weight = jnp.dot(features.T, back_rounded, preferred_element_type=jnp.float32) / math.sqrt(NODES)
    return (logits, grad_features, grad_weight)
```

```python
import functools
import math

import jax
import jax.numpy as jnp
from jax import lax
from jax.experimental import pallas as pl
from jax.experimental.pallas import tpu as pltpu
from jax.sharding import PartitionSpec as P

MESH = pl.DeviceIdType.MESH
F32 = jnp.float32
BF16 = jnp.bfloat16


def kernel(dims, features_h, weight_h, tiles, rows_h, cols_h, live, cot_h,
           logits, grad_features, grad_weight,
           features, weight, slot_rows, slot_cols,
           tile_buf, sums, dense, proj, cots, cots_t, feat_t, code_v, last_v, code, last,
           sib_out, sib_in, y_out, y_in, z_out, z_in, log_out, log_in,
           term_out, term_in, total,
           tile_sem, in_sem, smem_sem, cot_send, cot_recv, ag_send, ag_recv,
           sib_send, sib_recv, y_send, y_recv, z_send, z_recv,
           log_send, log_recv, term_send, term_recv, tot_send, tot_recv):
    R, C, O, I = dims
    n = R * C
    slots = tiles.shape[0]
    side = tiles.shape[1]
    stretch = features.shape[0]
    per = stretch // side
    row_tiles = R * per
    block_cells = row_tiles * per
    cells = C * block_cells
    r, c = lax.axis_index("row"), lax.axis_index("col")
    me = r * C + c
    k = lax.rem(c, 2)
    q = c // 2
    y = lax.rem(q, I)
    z = q // I

    def col_of(zz, yy, kk):
        return (zz * I + yy) * 2 + kk

    def remote(src, dst, send, recv, dev):
        return pltpu.make_async_remote_copy(
            src_ref=src, dst_ref=dst, send_sem=send, recv_sem=recv,
            device_id=dev, device_id_type=MESH)

    inputs = [
        pltpu.make_async_copy(src, dst, in_sem.at[i])
        for i, (src, dst) in enumerate((
            (rows_h, slot_rows), (cols_h, slot_cols),
            (features_h, features), (weight_h, weight), (cot_h, cots.at[r])))
    ]
    for copy in inputs:
        copy.start()
    chunks = tile_sem.shape[0]
    chunk = slots // chunks
    loads = [
        pltpu.make_async_copy(tiles.at[pl.ds(i * chunk, chunk)],
                              tile_buf.at[pl.ds(i * chunk, chunk)], tile_sem.at[i])
        for i in range(chunks)
    ]
    for load in loads[:0]:
        load.start()

    x_peers = [lax.rem(r + d, R) for d in range(1, R)]
    y_peers = [lax.rem(y + d, I) for d in range(1, I)]
    z_peers = [lax.rem(z + d, O) for d in range(1, O)]
    near = ([(peer, c) for peer in x_peers] + [(r, col_of(z, yy, k)) for yy in y_peers]
            + [(r, col_of(zz, y, k)) for zz in z_peers] + [(r, col_of(z, y, 1 - k))])
    barrier = pltpu.get_barrier_semaphore()
    with jax.named_scope("S00greet"):
        for dev in near:
            pl.semaphore_signal(barrier, inc=1, device_id=dev, device_id_type=MESH)

    with jax.named_scope("S01idx"):
        for copy in inputs[:2]:
            copy.wait()
    with jax.named_scope("S01rest"):
        for load in loads[0:]:
            load.start()
    with jax.named_scope("S02sort"):
        lane = lax.broadcasted_iota(jnp.int32, (1, slots), 1)
        col = slot_cols[...]
        where = (col // per) * block_cells + slot_rows[...] * per + lax.rem(col, per)
        cell = jnp.where(lane < live[0, 0], where, cells)
        eye = (lax.broadcasted_iota(jnp.int32, (slots, slots), 0)
               == lax.broadcasted_iota(jnp.int32, (slots, slots), 1))
        cell_c = jnp.sum(jnp.where(eye, cell, 0), axis=1, keepdims=True)
        sub = lax.broadcasted_iota(jnp.int32, (slots, 1), 0)
        before = (cell < cell_c) | ((cell == cell_c) & (lane < sub))
        rank = jnp.sum(before.astype(jnp.int32), axis=1, keepdims=True)
        code_v[...] = jnp.sum(jnp.where(rank == lane, sub, 0), axis=0, keepdims=True)
        cell_ids = lax.broadcasted_iota(jnp.int32, (1, cells + 128), 1)
        last_v[...] = jnp.sum((cell_c < cell_ids).astype(jnp.int32), axis=0, keepdims=True)
        to_smem = [pltpu.make_async_copy(code_v, code, smem_sem.at[0]),
                   pltpu.make_async_copy(last_v, last, smem_sem.at[1])]
        for copy in to_smem:
            copy.start()
    with jax.named_scope("S03proj"):
        for copy in inputs[2:]:
            copy.wait()
        proj[c] = jnp.dot(features[...], weight[...], preferred_element_type=F32).astype(BF16)
        feat_t[...] = features[...].astype(F32).T.astype(BF16)
        cots_t[r] = cots[r].astype(F32).T.astype(BF16)
        sums[0] = jnp.zeros((side, side), F32)
    with jax.named_scope("S04barrier"):
        pl.semaphore_wait(barrier, len(near))

    pending = []

    def gather_send(block, dev):
        copy = remote(proj.at[block], proj.at[block], ag_send.at[len(pending)],
                      ag_recv.at[block], (r, dev))
        copy.start()
        pending.append(copy)

    def gather_wait(block):
        remote(proj.at[block], proj.at[block], ag_send.at[0], ag_recv.at[block],
               (r, c)).wait_recv()

    cot_copies = []
    for d in range(1, R):
        copy = remote(cots.at[r], cots.at[r], cot_send.at[d], cot_recv.at[r], (x_peers[d - 1], c))
        copy.start()
        cot_copies.append(copy)
    for yy in y_peers:
        gather_send(c, col_of(z, yy, k))
    for zz in z_peers:
        gather_send(c, col_of(zz, y, k))
    gather_send(c, col_of(z, y, 1 - k))

    with jax.named_scope("S07loads"):
        for copy in to_smem:
            copy.wait()
        for load in loads:
            load.wait()

    def add_slot(j, acc):
        acc = acc + tile_buf[code[0, j]].astype(F32)
        sums[j + 1] = acc
        return acc

    def pass_on(zz):
        block = col_of(zz, y, k)
        gather_wait(block)
        for yy in y_peers:
            gather_send(block, col_of(z, yy, k))
        gather_send(block, col_of(z, y, 1 - k))

    parts = 8
    early = ()
    acc = jnp.zeros((side, side), F32)
    with jax.named_scope("S08sums"):
        for part in range(parts):
            acc = lax.fori_loop(part * slots // parts, (part + 1) * slots // parts, add_slot, acc,
                                unroll=8)
            for i, at in enumerate(early):
                if at == part and i < len(z_peers):
                    pass_on(z_peers[i])

    with jax.named_scope("S09cot"):
        for d in range(1, R):
            peer = x_peers[d - 1]
            remote(cots.at[peer], cots.at[peer], cot_send.at[d], cot_recv.at[peer], (peer, c)).wait_recv()
            cots_t[peer] = cots[peer].astype(F32).T.astype(BF16)

    kept = dense.shape[0] == C

    def row_block(b, t, start):
        base = b * block_cells + t * per
        parts = []
        for e in range(per):
            end = sums[last[0, base + e + 1]]
            parts.append((end - start).astype(BF16))
            start = end
        return parts, start

    def back_block(b):
        at = b if kept else 0
        start = sums[last[0, b * block_cells]]
        for t in range(row_tiles):
            parts, start = row_block(b, t, start)
            for e in range(per):
                dense[at, t * side:(t + 1) * side, e * side:(e + 1) * side] = parts[e]
        left = jnp.concatenate([cots_t[s] for s in range(R)], axis=1)
        return jnp.dot(left, dense[at], preferred_element_type=F32)

    def far_first(i):
        if O == 1:
            return z
        late = (2 * z) // O
        up = i + (i - z + O) // O
        down = O - 1 - i
        down = down - (z - down + O) // O
        return late * up + (1 - late) * down

    def z_order(i):
        own = i // (O - 1) if O > 1 else 1
        return own * z + (1 - own) * far_first(lax.rem(i, O - 1)) if O > 1 else z

    def place(i):
        return z_order(lax.rem(i, O)), lax.rem(y + i // O + 1, I)

    def sib_copy(m):
        return remote(sib_out.at[m], sib_in.at[m], sib_send.at[m], sib_recv.at[m],
                      (r, col_of(z, y, 1 - k)))

    def send_sib(i, carry):
        zz, yy = place(i)
        m = zz * I + yy
        sib_out[m] = back_block(2 * m + 1 - k).astype(BF16)
        sib_copy(m).start()
        return carry

    def y_copy(zz, yy):
        return remote(y_out.at[zz * I + yy], y_in.at[y * O + zz], y_send.at[zz * I + yy],
                      y_recv.at[y * O + zz], (r, col_of(z, yy, k)))

    def send_y(i, carry):
        zz, yy = place(i)
        m = zz * I + yy
        mine = back_block(2 * m + k)
        sib_copy(m).wait_recv()
        y_out[m] = (mine + sib_in[m].astype(F32)).astype(BF16)
        y_copy(zz, yy).start()
        return carry

    with jax.named_scope("S10sib"):
        lax.fori_loop(0, O * (I - 1), send_sib, 0)
    with jax.named_scope("S11y"):
        lax.fori_loop(0, O * (I - 1), send_y, 0)
    with jax.named_scope("S12agfwda"):
        for zz in z_peers[len(early):2]:
            pass_on(zz)
    with jax.named_scope("S12sib"):
        lax.fori_loop(O * (I - 1), O * I, send_sib, 0)
    with jax.named_scope("S12agfwdb"):
        for zz in z_peers[2:]:
            pass_on(zz)

    def summed(zz):
        m = zz * I + y
        value = back_block(2 * m + k)
        sib_copy(m).wait_recv()
        value = value + sib_in[m].astype(F32)
        for yy in y_peers:
            slot = yy * O + zz
            remote(y_out.at[0], y_in.at[slot], y_send.at[0], y_recv.at[slot],
                   (r, c)).wait_recv()
            value = value + y_in[slot].astype(F32)
        return value

    z_copies = []
    with jax.named_scope("S13z"):
        for d in range(O - 1):
            zz = z_order(d)
            z_out[d] = summed(zz).astype(BF16)
            copy = remote(z_out.at[d], z_in.at[z], z_send.at[d], z_recv.at[z],
                          (r, col_of(zz, y, k)))
            copy.start()
            z_copies.append(copy)
    with jax.named_scope("S17own"):
        back_t = summed(z)
    with jax.named_scope("S18zwait"):
        for zz in z_peers:
            remote(z_out.at[0], z_in.at[zz], z_send.at[0], z_recv.at[zz], (r, c)).wait_recv()
            back_t = back_t + z_in[zz].astype(F32)
    with jax.named_scope("S19term"):
        back = back_t.T.astype(BF16)
        term = jnp.dot(feat_t[...], back, preferred_element_type=F32)
        term_out[...] = term.reshape(term_out.shape).astype(BF16)

    owners = term_out.shape[0]
    z_low, z_count = ((O - 1) // 2, 2) if O % 2 == 0 else (O // 2, 1)
    group = z_count * I * 2

    def owner_device(o):
        kk = lax.rem(o, 2)
        yy = lax.rem(o // 2, I)
        zz = z_low + lax.rem(o // (2 * I), z_count)
        return o // group, col_of(zz, yy, kk)

    mine_o = ((r * z_count + z - z_low) * I + y) * 2 + k
    is_owner = (z >= z_low) & (z < z_low + z_count) & (mine_o < owners)

    def term_copy(o):
        return remote(term_out.at[o], term_in.at[me], term_send.at[0], term_recv.at[0],
                      owner_device(o))

    def bulk(count, send, recv):
        part = term_in.at[pl.ds(0, count)]
        return remote(part, part, send.at[0], recv.at[0], (r, c))

    def by_role(act):
        pl.when(is_owner)(lambda: act(owners - 1))
        pl.when(jnp.logical_not(is_owner))(lambda: act(owners))

    def tot_copy(t):
        return remote(total.at[mine_o], total.at[mine_o], tot_send.at[0], tot_recv.at[0],
                      (t // C, lax.rem(t, C)))

    with jax.named_scope("S20termsend"):
        @pl.when(is_owner)
        def _():
            def body(d, carry):
                term_copy(lax.rem(mine_o + d, owners)).start()
                return carry
            lax.fori_loop(1, owners, body, 0, unroll=owners - 1 if owners > 1 else 1)
            term_in[me] = term_out[mine_o]

        @pl.when(jnp.logical_not(is_owner))
        def _():
            def body(d, carry):
                term_copy(lax.rem(me + d, owners)).start()
                return carry
            lax.fori_loop(0, owners, body, 0, unroll=owners)

    with jax.named_scope("S21gf"):
        grad_features[...] = lax.dot_general(
            back, weight[...], (((1,), (1,)), ((), ())), preferred_element_type=F32).astype(BF16)

    with jax.named_scope("S22agfwd"):
        for d in range(O):
            zz = lax.rem(z + d, O)
            for yy in y_peers:
                block = col_of(zz, yy, k)
                gather_wait(block)
                gather_send(block, col_of(z, y, 1 - k))
    with jax.named_scope("S23agwait"):
        for d in range(O):
            for e in range(I):
                gather_wait(col_of(lax.rem(z + d, O), lax.rem(y + e, I), 1 - k))

    wide = 4 if C % 4 == 0 else 1

    def forward(s):
        rows_of = pl.ds(pl.multiple_of(s * stretch, stretch), stretch)

        def stretch_block(b):
            if kept:
                return dense[b, rows_of, :]
            blocks = []
            for a in range(per):
                t = s * per + a
                parts, _ = row_block(b, t, sums[last[0, b * block_cells + t * per]])
                blocks.append(jnp.concatenate(parts, axis=1))
            return jnp.concatenate(blocks, axis=0)

        def step(g, out):
            left = jnp.concatenate([stretch_block(g * wide + b) for b in range(wide)], axis=1)
            right = jnp.concatenate([proj[g * wide + b] for b in range(wide)], axis=0)
            return out + jnp.dot(left, right, preferred_element_type=F32)
        return lax.fori_loop(0, C // wide, step, jnp.zeros((stretch, proj.shape[2]), F32))

    log_copies = []
    with jax.named_scope("S24fwdpeer"):
        for d in range(1, R):
            peer = x_peers[d - 1]
            log_out[d - 1] = forward(peer).astype(BF16)
            copy = remote(log_out.at[d - 1], log_in.at[r], log_send.at[d], log_recv.at[r], (peer, c))
            copy.start()
            log_copies.append(copy)

    with jax.named_scope("S25own"):
        @pl.when(is_owner)
        def _():
            bulk(n - 1, term_send, term_recv).wait_recv()
            whole = jnp.sum(term_in[...].astype(F32), axis=0) * (1.0 / math.sqrt(n * stretch))
            total[mine_o] = whole.astype(BF16)

            def body(d, carry):
                tot_copy(lax.rem(me + d, n)).start()
                return carry
            lax.fori_loop(1, n, body, 0, unroll=n - 1 if n <= 32 else 1)

    with jax.named_scope("S26fwdme"):
        mine_log = forward(r)
    with jax.named_scope("S27log"):
        for d in range(1, R):
            peer = x_peers[d - 1]
            remote(log_out.at[0], log_in.at[peer], log_send.at[0], log_recv.at[peer],
                   (peer, c)).wait_recv()
            mine_log = mine_log + log_in[peer].astype(F32)
        logits[...] = mine_log.astype(BF16)
    with jax.named_scope("S28drain"):
        for copy in pending + cot_copies + log_copies + z_copies:
            copy.wait_send()

        def drain_sib(m, carry):
            sib_copy(m).wait_send()
            return carry

        lax.fori_loop(0, O * I, drain_sib, 0)

        def drain_y(i, carry):
            zz, yy = place(i)
            y_copy(zz, yy).wait_send()
            return carry

        lax.fori_loop(0, O * (I - 1), drain_y, 0)
        by_role(lambda count: bulk(count, term_send, term_recv).wait_send())
    with jax.named_scope("S29totwait"):
        by_role(lambda count: bulk(count, tot_send, tot_recv).wait_recv())
    with jax.named_scope("S30end"):
        grad_weight[...] = total[...].astype(F32).reshape(grad_weight.shape)

        @pl.when(is_owner)
        def _():
            bulk(n - 1, tot_send, tot_recv).wait_send()


def hand_over(a, b, c, x, y, z):
    x[...] = a[...]
    y[...] = b[...]
    z[...] = c[...]


def per_device(R, C, features, weight, tiles, slot_tile_row, tile_cols, live_tiles, cotangent):
    slots, side = tiles.shape[2], tiles.shape[3]
    stretch, width = features.shape
    out_width = weight.shape[1]
    half = C // 2
    O = 4 if half % 4 == 0 else half
    I = half // O
    n = R * C
    per = stretch // side
    cells = R * per * C * per
    centre = R * (2 if O % 2 == 0 else 1) * I * 2
    owners = min(centre, width // 16)
    rows = width // owners
    chunks = 8 if slots % 8 == 0 else 1
    dma = pltpu.SemaphoreType.DMA
    vmem = pltpu.VMEM
    blk = (out_width, stretch)
    gathers = (O - 1) + (I - 1) + 1 + (O - 1) * I + O * (I - 1)
    scratch = [
        vmem((stretch, width), BF16),
        vmem((width, out_width), BF16),
        vmem((1, slots), jnp.int32),
        vmem((1, slots), jnp.int32),
        vmem((slots, side, side), BF16),
        vmem((slots + 1, side, side), F32),
        vmem((C if C * R <= 64 else 1, R * stretch, stretch), BF16),
        vmem((C, stretch, out_width), BF16),
        vmem((R, stretch, out_width), BF16),
        vmem((R,) + blk, BF16),
        vmem((width, stretch), BF16),
        vmem((1, slots), jnp.int32),
        vmem((1, cells + 128), jnp.int32),
        pltpu.SMEM((1, slots), jnp.int32),
        pltpu.SMEM((1, cells + 128), jnp.int32),
        vmem((half,) + blk, BF16),
        vmem((half,) + blk, BF16),
        vmem((half,) + blk, BF16),
        vmem((half,) + blk, BF16),
        vmem((max(O - 1, 1),) + blk, BF16),
        vmem((O,) + blk, BF16),
        vmem((max(R - 1, 1), stretch, out_width), BF16),
        vmem((R, stretch, out_width), BF16),
        vmem((owners, rows, out_width), BF16),
        vmem((n, rows, out_width), BF16),
        vmem((owners, rows, out_width), BF16),
        dma((chunks,)), dma((5,)), dma((2,)), dma((R,)), dma((R,)),
        dma((gathers,)), dma((C,)),
        dma((half,)), dma((half,)), dma((half,)), dma((half,)),
        dma((O,)), dma((O,)), dma((R,)), dma((R,)),
        dma((1,)), dma((1,)), dma((1,)), dma((1,)),
    ]
    v = pl.BlockSpec(memory_space=pltpu.VMEM)
    hbm = pl.BlockSpec(memory_space=pltpu.HBM)
    shapes = (
            jax.ShapeDtypeStruct((stretch, out_width), BF16),
            jax.ShapeDtypeStruct((stretch, width), BF16),
            jax.ShapeDtypeStruct((width, out_width), F32),
        )

    def in_hbm(x):
        return pltpu.with_memory_space_constraint(x, pltpu.HBM)

    results = pl.pallas_call(
        functools.partial(kernel, (R, C, O, I)),
        out_shape=tuple(vmem(s.shape, s.dtype) for s in shapes),
        in_specs=[hbm] * 5 + [pl.BlockSpec(memory_space=pltpu.SMEM), hbm],
        out_specs=(v, v, v),
        scratch_shapes=scratch,
        compiler_params=pltpu.CompilerParams(
            collective_id=0, has_side_effects=True, vmem_limit_bytes=52 * 1024 * 1024),
    )(in_hbm(features), in_hbm(weight), in_hbm(tiles.reshape(slots, side, side)),
      in_hbm(slot_tile_row.reshape(1, slots)), in_hbm(tile_cols.reshape(1, slots)), live_tiles,
      in_hbm(cotangent))
    results = [pltpu.with_memory_space_constraint(x, pltpu.VMEM) for x in results]
    return pl.pallas_call(hand_over, out_shape=shapes, in_specs=[v, v, v],
                          out_specs=(v, v, v))(*results)


def solution(mesh):
    R, C = mesh.shape["row"], mesh.shape["col"]
    placed = (
        P(("row", "col"), None),
        P(),
        P("row", "col", None, None, None),
        P("row", "col", None),
        P("row", "col", None),
        P("row", "col"),
        P(("row", "col"), None),
    )
    return jax.shard_map(
        functools.partial(per_device, R, C),
        mesh=mesh,
        in_specs=placed,
        out_specs=(P(("row", "col"), None), P(("row", "col"), None), P()),
        check_vma=False,
    )
```

```python
import functools
import math

import jax
import jax.numpy as jnp
from jax import lax
from jax.experimental import pallas as pl
from jax.experimental.pallas import tpu as pltpu
from jax.sharding import PartitionSpec as P

MESH = pl.DeviceIdType.MESH
F32 = jnp.float32
BF16 = jnp.bfloat16


def kernel(dims, features_h, weight_h, tiles, rows_h, cols_h, live, cot_h,
           logits, grad_features, grad_weight,
           features, weight, slot_rows, slot_cols,
           tile_buf, sums, dense, proj, cots, cots_t, feat_t, code_v, last_v, code, last,
           sib_out, sib_in, y_out, y_in, p_out, p_in, z_out, z_in, log_out, log_in, far_feat,
           term_out, term_in, total,
           tile_sem, in_sem, smem_sem, cot_send, cot_recv, ag_send, ag_recv,
           sib_send, sib_recv, y_send, y_recv, p_send, p_recv, z_send, z_recv, far_send, far_recv,
           log_send, log_recv, term_send, term_recv, tot_send, tot_recv):
    R, C, O, I = dims
    n = R * C
    slots = tiles.shape[0]
    side = tiles.shape[1]
    stretch = features.shape[0]
    per = stretch // side
    row_tiles = R * per
    block_cells = row_tiles * per
    cells = C * block_cells
    r, c = lax.axis_index("row"), lax.axis_index("col")
    me = r * C + c
    k = lax.rem(c, 2)
    q = c // 2
    y = lax.rem(q, I)
    z = q // I
    H = O // 2
    zl = lax.rem(z, 2)
    zh = z // 2

    def col_of(zz, yy, kk):
        return (zz * I + yy) * 2 + kk

    def remote(src, dst, send, recv, dev):
        return pltpu.make_async_remote_copy(
            src_ref=src, dst_ref=dst, send_sem=send, recv_sem=recv,
            device_id=dev, device_id_type=MESH)

    inputs = [
        pltpu.make_async_copy(src, dst, in_sem.at[i])
        for i, (src, dst) in enumerate((
            (rows_h, slot_rows), (cols_h, slot_cols),
            (features_h, features), (weight_h, weight), (cot_h, cots.at[r])))
    ]
    for copy in inputs:
        copy.start()
    chunks = tile_sem.shape[0]
    chunk = slots // chunks
    loads = [
        pltpu.make_async_copy(tiles.at[pl.ds(i * chunk, chunk)],
                              tile_buf.at[pl.ds(i * chunk, chunk)], tile_sem.at[i])
        for i in range(chunks)
    ]
    for load in loads[:0]:
        load.start(priority=0)

    x_peers = [lax.rem(r + d, R) for d in range(1, R)]
    y_peers = [lax.rem(y + d, I) for d in range(1, I)]
    partner = 2 * zh + 1 - zl
    odd_peers = [2 * lax.rem(zh + d, H) + 1 - zl for d in range(H)]
    even_peers = [2 * lax.rem(zh + d, H) + zl for d in range(1, H)]
    z_peers = odd_peers + even_peers
    near = ([(peer, c) for peer in x_peers] + [(r, col_of(z, yy, k)) for yy in y_peers]
            + [(r, col_of(zz, y, k)) for zz in z_peers] + [(r, col_of(z, y, 1 - k))])
    barrier = pltpu.get_barrier_semaphore()
    with jax.named_scope("S00greet"):
        for dev in near:
            pl.semaphore_signal(barrier, inc=1, device_id=dev, device_id_type=MESH)

    with jax.named_scope("S01idx"):
        for copy in inputs[:2]:
            copy.wait()
    with jax.named_scope("S01rest"):
        for load in loads[0:]:
            load.start(priority=0)
    with jax.named_scope("S02sort"):
        lane = lax.broadcasted_iota(jnp.int32, (1, slots), 1)
        col = slot_cols[...]
        where = (col // per) * block_cells + slot_rows[...] * per + lax.rem(col, per)
        cell = jnp.where(lane < live[0, 0], where, cells)
        eye = (lax.broadcasted_iota(jnp.int32, (slots, slots), 0)
               == lax.broadcasted_iota(jnp.int32, (slots, slots), 1))
        cell_c = jnp.sum(jnp.where(eye, cell, 0), axis=1, keepdims=True)
        sub = lax.broadcasted_iota(jnp.int32, (slots, 1), 0)
        before = (cell < cell_c) | ((cell == cell_c) & (lane < sub))
        rank = jnp.sum(before.astype(jnp.int32), axis=1, keepdims=True)
        code_v[...] = jnp.sum(jnp.where(rank == lane, sub, 0), axis=0, keepdims=True)
        cell_ids = lax.broadcasted_iota(jnp.int32, (1, cells + 128), 1)
        last_v[...] = jnp.sum((cell_c < cell_ids).astype(jnp.int32), axis=0, keepdims=True)
        to_smem = [pltpu.make_async_copy(code_v, code, smem_sem.at[0]),
                   pltpu.make_async_copy(last_v, last, smem_sem.at[1])]
        for copy in to_smem:
            copy.start()
    with jax.named_scope("S03proj"):
        for copy in inputs[2:]:
            copy.wait()
        proj[c] = jnp.dot(features[...], weight[...], preferred_element_type=F32).astype(BF16)
        feat_t[0] = features[...].astype(F32).T.astype(BF16)
        cots_t[r] = cots[r].astype(F32).T.astype(BF16)
        sums[0] = jnp.zeros((side, side), F32)
    with jax.named_scope("S04barrier"):
        pl.semaphore_wait(barrier, len(near))

    pending = []
    pending_far = []

    def gather_send(block, dev):
        copy = remote(proj.at[block], proj.at[block], ag_send.at[len(pending)],
                      ag_recv.at[block], (r, dev))
        copy.start(priority=0)
        pending.append(copy)

    def gather_wait(block):
        remote(proj.at[block], proj.at[block], ag_send.at[0], ag_recv.at[block],
               (r, c)).wait_recv()

    cot_copies = []
    for d in range(1, R):
        copy = remote(cots.at[r], cots.at[r], cot_send.at[d], cot_recv.at[r], (x_peers[d - 1], c))
        copy.start(priority=0)
        cot_copies.append(copy)
    for yy in y_peers:
        gather_send(c, col_of(z, yy, k))
    for zz in odd_peers:
        gather_send(c, col_of(zz, y, k))
    for i, zz in enumerate(even_peers):
        copy = remote(features, far_feat.at[zh], far_send.at[i], far_recv.at[zh], (r, col_of(zz, y, k)))
        copy.start(priority=0)
        pending_far.append(copy)
    gather_send(c, col_of(z, y, 1 - k))

    with jax.named_scope("S07loads"):
        for copy in to_smem:
            copy.wait()
        for load in loads:
            load.wait()

    def add_slot(j, acc):
        acc = acc + tile_buf[code[0, j]].astype(F32)
        sums[j + 1] = acc
        return acc

    def pass_on(i):
        zz = z_peers[i]
        block = col_of(zz, y, k)
        if i < H:
            gather_wait(block)
        else:
            hh = lax.rem(zh + i - H + 1, H)
            remote(features, far_feat.at[hh], far_send.at[0], far_recv.at[hh], (r, c)).wait_recv()
            proj[block] = jnp.dot(far_feat[hh], weight[...], preferred_element_type=F32).astype(BF16)
            feat_t[i - H + 1] = far_feat[hh].astype(F32).T.astype(BF16)
        for yy in y_peers:
            gather_send(block, col_of(z, yy, k))
        gather_send(block, col_of(z, y, 1 - k))

    parts = 8
    early = (7,)
    acc = jnp.zeros((side, side), F32)
    with jax.named_scope("S08sums"):
        for part in range(parts):
            acc = lax.fori_loop(part * slots // parts, (part + 1) * slots // parts, add_slot, acc,
                                unroll=8)
            for i, at in enumerate(early):
                if at == part and i < len(z_peers):
                    pass_on(i)

    with jax.named_scope("S09cot"):
        for d in range(1, R):
            peer = x_peers[d - 1]
            remote(cots.at[peer], cots.at[peer], cot_send.at[d], cot_recv.at[peer], (peer, c)).wait_recv()
            cots_t[peer] = cots[peer].astype(F32).T.astype(BF16)

    kept = dense.shape[0] == C

    def row_block(b, t, start):
        base = b * block_cells + t * per
        parts = []
        for e in range(per):
            end = sums[last[0, base + e + 1]]
            parts.append((end - start).astype(BF16))
            start = end
        return parts, start

    def back_block(b):
        at = b if kept else 0
        start = sums[last[0, b * block_cells]]
        for t in range(row_tiles):
            parts, start = row_block(b, t, start)
            for e in range(per):
                dense[at, t * side:(t + 1) * side, e * side:(e + 1) * side] = parts[e]
        left = jnp.concatenate([cots_t[s] for s in range(R)], axis=1)
        return jnp.dot(left, dense[at], preferred_element_type=F32)

    def z_order(i):
        late = i // H
        same = late * zl + (1 - late) * (1 - zl)
        return 2 * lax.rem(zh + 1 + lax.rem(i, H), H) + same

    def place(i):
        return z_order(lax.rem(i, O)), lax.rem(y + i // O + 1, I)

    def sib_copy(m):
        return remote(sib_out.at[m], sib_in.at[m], sib_send.at[m], sib_recv.at[m],
                      (r, col_of(z, y, 1 - k)))

    def send_sib(i, carry):
        zz, yy = place(i)
        m = zz * I + yy
        sib_out[m] = back_block(2 * m + 1 - k).astype(BF16)
        sib_copy(m).start()
        return carry

    def y_copy(zz, yy):
        return remote(y_out.at[zz * I + yy], y_in.at[y * O + zz], y_send.at[zz * I + yy],
                      y_recv.at[y * O + zz], (r, col_of(z, yy, k)))

    def send_y(i, carry):
        zz, yy = place(i)
        m = zz * I + yy
        mine = back_block(2 * m + k)
        sib_copy(m).wait_recv()
        y_out[m] = (mine + sib_in[m].astype(F32)).astype(BF16)
        y_copy(zz, yy).start()
        return carry

    with jax.named_scope("S10sib"):
        lax.fori_loop(0, O * (I - 1), send_sib, 0)
    with jax.named_scope("S11y"):
        lax.fori_loop(0, O * (I - 1), send_y, 0)
    with jax.named_scope("S12agfwda"):
        for i in range(len(early), 2):
            pass_on(i)
    with jax.named_scope("S12sib"):
        lax.fori_loop(O * (I - 1), O * I, send_sib, 0)
    with jax.named_scope("S12agfwdb"):
        for i in range(max(2, len(early)), O - 1):
            pass_on(i)

    def summed(zz):
        m = zz * I + y
        value = back_block(2 * m + k)
        sib_copy(m).wait_recv()
        value = value + sib_in[m].astype(F32)
        for yy in y_peers:
            slot = yy * O + zz
            remote(y_out.at[0], y_in.at[slot], y_send.at[0], y_recv.at[slot],
                   (r, c)).wait_recv()
            value = value + y_in[slot].astype(F32)
        return value

    z_copies = []
    with jax.named_scope("S13p"):
        for i in range(H):
            hh = lax.rem(zh + 1 + i, H)
            p_out[i] = summed(z_order(i)).astype(BF16)
            copy = remote(p_out.at[i], p_in.at[hh], p_send.at[i], p_recv.at[hh],
                          (r, col_of(partner, y, k)))
            copy.start()
            z_copies.append(copy)
    lefts, rights = [feat_t[0]], []
    for i in range(H):
        with jax.named_scope("S14own"):
            hh = lax.rem(zh + 1 + i, H)
            value = summed(z_order(H + i))
        with jax.named_scope("S15pwait"):
            remote(p_out.at[0], p_in.at[hh], p_send.at[0], p_recv.at[hh], (r, c)).wait_recv()
            value = value + p_in[hh].astype(F32)
            if i < H - 1:
                z_out[i] = value.astype(BF16)
                copy = remote(z_out.at[i], z_in.at[zh], z_send.at[i], z_recv.at[zh],
                              (r, col_of(2 * hh + zl, y, k)))
                copy.start()
                z_copies.append(copy)
                lefts.append(feat_t[i + 1])
                rights.append(value.T.astype(BF16))
    with jax.named_scope("S19term"):
        back_t = value
        rights = [value.T.astype(BF16)] + rights
        term = jnp.dot(jnp.concatenate(lefts, axis=1), jnp.concatenate(rights, axis=0),
                       preferred_element_type=F32)
        term_out[...] = term.reshape(term_out.shape).astype(BF16)

    owners = term_out.shape[0]
    z_low, z_count = H - 1, 2
    group = z_count * I * 2

    def owner_device(o):
        kk = lax.rem(o, 2)
        yy = lax.rem(o // 2, I)
        zz = z_low + lax.rem(o // (2 * I), z_count)
        return o // group, col_of(zz, yy, kk)

    mine_o = ((r * z_count + z - z_low) * I + y) * 2 + k
    is_owner = (z >= z_low) & (z < z_low + z_count) & (mine_o < owners)

    def term_copy(o):
        return remote(term_out.at[o], term_in.at[me], term_send.at[0], term_recv.at[0],
                      owner_device(o))

    def bulk(count, send, recv):
        part = term_in.at[pl.ds(0, count)]
        return remote(part, part, send.at[0], recv.at[0], (r, c))

    def by_role(act):
        pl.when(is_owner)(lambda: act(owners - 1))
        pl.when(jnp.logical_not(is_owner))(lambda: act(owners))

    def tot_copy(t):
        return remote(total.at[mine_o], total.at[mine_o], tot_send.at[0], tot_recv.at[0],
                      (t // C, lax.rem(t, C)))

    with jax.named_scope("S20termsend"):
        @pl.when(is_owner)
        def _():
            def body(d, carry):
                term_copy(lax.rem(mine_o + d, owners)).start()
                return carry
            lax.fori_loop(1, owners, body, 0, unroll=owners - 1 if owners > 1 else 1)
            term_in[me] = term_out[mine_o]

        @pl.when(jnp.logical_not(is_owner))
        def _():
            def body(d, carry):
                term_copy(lax.rem(me + d, owners)).start()
                return carry
            lax.fori_loop(0, owners, body, 0, unroll=owners)

    with jax.named_scope("S22agfwd"):
        for d in range(O):
            zz = lax.rem(z + d, O)
            for yy in y_peers:
                block = col_of(zz, yy, k)
                gather_wait(block)
                gather_send(block, col_of(z, y, 1 - k))
    with jax.named_scope("S23agwait"):
        for d in range(O):
            for e in range(I):
                gather_wait(col_of(lax.rem(z + d, O), lax.rem(y + e, I), 1 - k))

    wide = 4 if C % 4 == 0 else 1

    def forward(s):
        rows_of = pl.ds(pl.multiple_of(s * stretch, stretch), stretch)

        def stretch_block(b):
            if kept:
                return dense[b, rows_of, :]
            blocks = []
            for a in range(per):
                t = s * per + a
                parts, _ = row_block(b, t, sums[last[0, b * block_cells + t * per]])
                blocks.append(jnp.concatenate(parts, axis=1))
            return jnp.concatenate(blocks, axis=0)

        def step(g, out):
            left = jnp.concatenate([stretch_block(g * wide + b) for b in range(wide)], axis=1)
            right = jnp.concatenate([proj[g * wide + b] for b in range(wide)], axis=0)
            return out + jnp.dot(left, right, preferred_element_type=F32)
        return lax.fori_loop(0, C // wide, step, jnp.zeros((stretch, proj.shape[2]), F32))

    log_copies = []
    with jax.named_scope("S24fwdpeer"):
        for d in range(1, R):
            peer = x_peers[d - 1]
            log_out[d - 1] = forward(peer).astype(BF16)
            copy = remote(log_out.at[d - 1], log_in.at[r], log_send.at[d], log_recv.at[r], (peer, c))
            copy.start()
            log_copies.append(copy)

    with jax.named_scope("S25own"):
        @pl.when(is_owner)
        def _():
            bulk(n - 1, term_send, term_recv).wait_recv()
            whole = jnp.sum(term_in[...].astype(F32), axis=0) * (1.0 / math.sqrt(n * stretch))
            total[mine_o] = whole.astype(BF16)

            def body(d, carry):
                tot_copy(lax.rem(me + d, n)).start()
                return carry
            lax.fori_loop(1, n, body, 0, unroll=n - 1 if n <= 32 else 1)

    with jax.named_scope("S26gf"):
        for i in range(H - 1):
            hh = lax.rem(zh + 1 + i, H)
            remote(z_out.at[0], z_in.at[hh], z_send.at[0], z_recv.at[hh], (r, c)).wait_recv()
            back_t = back_t + z_in[hh].astype(F32)
        grad_features[...] = lax.dot_general(
            back_t.T.astype(BF16), weight[...], (((1,), (1,)), ((), ())),
            preferred_element_type=F32).astype(BF16)

    with jax.named_scope("S26fwdme"):
        mine_log = forward(r)
    with jax.named_scope("S27log"):
        for d in range(1, R):
            peer = x_peers[d - 1]
            remote(log_out.at[0], log_in.at[peer], log_send.at[0], log_recv.at[peer],
                   (peer, c)).wait_recv()
            mine_log = mine_log + log_in[peer].astype(F32)
        logits[...] = mine_log.astype(BF16)
    with jax.named_scope("S28drain"):
        for copy in pending + pending_far + cot_copies + log_copies + z_copies:
            copy.wait_send()

        def drain_sib(m, carry):
            sib_copy(m).wait_send()
            return carry

        lax.fori_loop(0, O * I, drain_sib, 0)

        def drain_y(i, carry):
            zz, yy = place(i)
            y_copy(zz, yy).wait_send()
            return carry

        lax.fori_loop(0, O * (I - 1), drain_y, 0)
        by_role(lambda count: bulk(count, term_send, term_recv).wait_send())
    with jax.named_scope("S29totwait"):
        by_role(lambda count: bulk(count, tot_send, tot_recv).wait_recv())
    with jax.named_scope("S30end"):
        grad_weight[...] = total[...].astype(F32).reshape(grad_weight.shape)

        @pl.when(is_owner)
        def _():
            bulk(n - 1, tot_send, tot_recv).wait_send()


def hand_over(a, b, c, x, y, z):
    x[...] = a[...]
    y[...] = b[...]
    z[...] = c[...]


def per_device(R, C, features, weight, tiles, slot_tile_row, tile_cols, live_tiles, cotangent):
    slots, side = tiles.shape[2], tiles.shape[3]
    stretch, width = features.shape
    out_width = weight.shape[1]
    half = C // 2
    O = 4 if half % 4 == 0 else 2
    H = O // 2
    I = half // O
    n = R * C
    per = stretch // side
    cells = R * per * C * per
    centre = R * 2 * I * 2
    owners = min(centre, width // 16)
    rows = width // owners
    chunks = 8 if slots % 8 == 0 else 1
    dma = pltpu.SemaphoreType.DMA
    vmem = pltpu.VMEM
    blk = (out_width, stretch)
    gathers = (O - 1) + (I - 1) + 1 + (O - 1) * I + O * (I - 1)
    scratch = [
        vmem((stretch, width), BF16),
        vmem((width, out_width), BF16),
        vmem((1, slots), jnp.int32),
        vmem((1, slots), jnp.int32),
        vmem((slots, side, side), BF16),
        vmem((slots + 1, side, side), F32),
        vmem((C if C * R <= 64 else 1, R * stretch, stretch), BF16),
        vmem((C, stretch, out_width), BF16),
        vmem((R, stretch, out_width), BF16),
        vmem((R,) + blk, BF16),
        vmem((H, width, stretch), BF16),
        vmem((1, slots), jnp.int32),
        vmem((1, cells + 128), jnp.int32),
        pltpu.SMEM((1, slots), jnp.int32),
        pltpu.SMEM((1, cells + 128), jnp.int32),
        vmem((half,) + blk, BF16),
        vmem((half,) + blk, BF16),
        vmem((half,) + blk, BF16),
        vmem((half,) + blk, BF16),
        vmem((H,) + blk, BF16),
        vmem((H,) + blk, BF16),
        vmem((H,) + blk, BF16),
        vmem((H,) + blk, BF16),
        vmem((max(R - 1, 1), stretch, out_width), BF16),
        vmem((R, stretch, out_width), BF16),
        vmem((H, stretch, width), BF16),
        vmem((owners, rows, out_width), BF16),
        vmem((n, rows, out_width), BF16),
        vmem((owners, rows, out_width), BF16),
        dma((chunks,)), dma((5,)), dma((2,)), dma((R,)), dma((R,)),
        dma((gathers,)), dma((C,)),
        dma((half,)), dma((half,)), dma((half,)), dma((half,)),
        dma((H,)), dma((H,)), dma((H,)), dma((H,)), dma((H,)), dma((H,)), dma((R,)), dma((R,)),
        dma((1,)), dma((1,)), dma((1,)), dma((1,)),
    ]
    v = pl.BlockSpec(memory_space=pltpu.VMEM)
    hbm = pl.BlockSpec(memory_space=pltpu.HBM)
    shapes = (
            jax.ShapeDtypeStruct((stretch, out_width), BF16),
            jax.ShapeDtypeStruct((stretch, width), BF16),
            jax.ShapeDtypeStruct((width, out_width), F32),
        )

    def in_hbm(x):
        return pltpu.with_memory_space_constraint(x, pltpu.HBM)

    results = pl.pallas_call(
        functools.partial(kernel, (R, C, O, I)),
        out_shape=tuple(vmem(s.shape, s.dtype) for s in shapes),
        in_specs=[hbm] * 5 + [pl.BlockSpec(memory_space=pltpu.SMEM), hbm],
        out_specs=(v, v, v),
        scratch_shapes=scratch,
        compiler_params=pltpu.CompilerParams(
            collective_id=0, has_side_effects=True, vmem_limit_bytes=52 * 1024 * 1024),
    )(in_hbm(features), in_hbm(weight), in_hbm(tiles.reshape(slots, side, side)),
      in_hbm(slot_tile_row.reshape(1, slots)), in_hbm(tile_cols.reshape(1, slots)), live_tiles,
      in_hbm(cotangent))
    results = [pltpu.with_memory_space_constraint(x, pltpu.VMEM) for x in results]
    return pl.pallas_call(hand_over, out_shape=shapes, in_specs=[v, v, v],
                          out_specs=(v, v, v))(*results)


def solution(mesh):
    R, C = mesh.shape["row"], mesh.shape["col"]
    placed = (
        P(("row", "col"), None),
        P(),
        P("row", "col", None, None, None),
        P("row", "col", None),
        P("row", "col", None),
        P("row", "col"),
        P(("row", "col"), None),
    )
    return jax.shard_map(
        functools.partial(per_device, R, C),
        mesh=mesh,
        in_specs=placed,
        out_specs=(P(("row", "col"), None), P(("row", "col"), None), P()),
        check_vma=False,
    )
```

```python
import functools
import math

import jax
import jax.numpy as jnp
from jax import lax
from jax.experimental import pallas as pl
from jax.experimental.pallas import tpu as pltpu
from jax.sharding import PartitionSpec as P

MESH = pl.DeviceIdType.MESH
F32 = jnp.float32
BF16 = jnp.bfloat16


def kernel(dims, features_h, weight_h, tiles, rows_h, cols_h, live, cot_h,
           logits, grad_features, grad_weight,
           features, weight, slot_rows, slot_cols,
           tile_buf, sums, dense, proj, cots, cots_t, feat_t, code_v, last_v, code, last,
           sib_out, sib_in, y_out, y_in, p_out, p_in, z_out, z_in, log_out, log_in, far_feat,
           term_out, term_in, total,
           tile_sem, in_sem, smem_sem, cot_send, cot_recv, ag_send, ag_recv,
           sib_send, sib_recv, y_send, y_recv, p_send, p_recv, z_send, z_recv, far_send, far_recv,
           log_send, log_recv, term_send, term_recv, tot_send, tot_recv):
    R, C, O, I = dims
    n = R * C
    slots = tiles.shape[0]
    side = tiles.shape[1]
    stretch = features.shape[0]
    per = stretch // side
    row_tiles = R * per
    block_cells = row_tiles * per
    cells = C * block_cells
    r, c = lax.axis_index("row"), lax.axis_index("col")
    me = r * C + c
    k = lax.rem(c, 2)
    q = c // 2
    y = lax.rem(q, I)
    z = q // I
    H = O // 2
    zl = lax.rem(z, 2)
    zh = z // 2

    def col_of(zz, yy, kk):
        return (zz * I + yy) * 2 + kk

    def remote(src, dst, send, recv, dev):
        return pltpu.make_async_remote_copy(
            src_ref=src, dst_ref=dst, send_sem=send, recv_sem=recv,
            device_id=dev, device_id_type=MESH)

    inputs = [
        pltpu.make_async_copy(src, dst, in_sem.at[i])
        for i, (src, dst) in enumerate((
            (rows_h, slot_rows), (cols_h, slot_cols),
            (features_h, features), (weight_h, weight), (cot_h, cots.at[r])))
    ]
    for copy in inputs:
        copy.start()
    chunks = tile_sem.shape[0]
    chunk = slots // chunks
    loads = [
        pltpu.make_async_copy(tiles.at[pl.ds(i * chunk, chunk)],
                              tile_buf.at[pl.ds(i * chunk, chunk)], tile_sem.at[i])
        for i in range(chunks)
    ]
    for load in loads[:8]:
        load.start(priority=1)

    x_peers = [lax.rem(r + d, R) for d in range(1, R)]
    y_peers = [lax.rem(y + d, I) for d in range(1, I)]
    partner = 2 * zh + 1 - zl
    odd_peers = [2 * lax.rem(zh + d, H) + 1 - zl for d in range(H)]
    even_peers = [2 * lax.rem(zh + d, H) + zl for d in range(1, H)]
    z_peers = odd_peers + even_peers
    z_near = z_peers
    near = ([(peer, c) for peer in x_peers] + [(r, col_of(z, yy, k)) for yy in y_peers]
            + [(r, col_of(zz, y, k)) for zz in z_near] + [(r, col_of(z, y, 1 - k))])
    barrier = pltpu.get_barrier_semaphore()
    with jax.named_scope("S00greet"):
        for dev in near:
            pl.semaphore_signal(barrier, inc=1, device_id=dev, device_id_type=MESH)

    with jax.named_scope("S01idx"):
        for copy in inputs[:2]:
            copy.wait()
    with jax.named_scope("S01rest"):
        for load in loads[8:8]:
            load.start(priority=1)
    with jax.named_scope("S02sort"):
        lane = lax.broadcasted_iota(jnp.int32, (1, slots), 1)
        col = slot_cols[...]
        where = (col // per) * block_cells + slot_rows[...] * per + lax.rem(col, per)
        cell = jnp.where(lane < live[0, 0], where, cells)
        eye = (lax.broadcasted_iota(jnp.int32, (slots, slots), 0)
               == lax.broadcasted_iota(jnp.int32, (slots, slots), 1))
        cell_c = jnp.sum(jnp.where(eye, cell, 0), axis=1, keepdims=True)
        sub = lax.broadcasted_iota(jnp.int32, (slots, 1), 0)
        before = (cell < cell_c) | ((cell == cell_c) & (lane < sub))
        rank = jnp.sum(before.astype(jnp.int32), axis=1, keepdims=True)
        code_v[...] = jnp.sum(jnp.where(rank == lane, sub, 0), axis=0, keepdims=True)
        cell_ids = lax.broadcasted_iota(jnp.int32, (1, cells + 128), 1)
        last_v[...] = jnp.sum((cell_c < cell_ids).astype(jnp.int32), axis=0, keepdims=True)
        to_smem = [pltpu.make_async_copy(code_v, code, smem_sem.at[0]),
                   pltpu.make_async_copy(last_v, last, smem_sem.at[1])]
        for copy in to_smem:
            copy.start()
    with jax.named_scope("S03proj"):
        for copy in inputs[2:]:
            copy.wait()
        proj[c] = jnp.dot(features[...], weight[...], preferred_element_type=F32).astype(BF16)
        feat_t[0] = features[...].astype(F32).T.astype(BF16)
        cots_t[r] = cots[r].astype(F32).T.astype(BF16)
        sums[0] = jnp.zeros((side, side), F32)
    with jax.named_scope("S04barrier"):
        pl.semaphore_wait(barrier, len(near))

    pending = []
    pending_far = []

    def gather_send(block, dev):
        copy = remote(proj.at[block], proj.at[block], ag_send.at[len(pending)],
                      ag_recv.at[block], (r, dev))
        copy.start(priority=0)
        pending.append(copy)

    def gather_wait(block):
        remote(proj.at[block], proj.at[block], ag_send.at[0], ag_recv.at[block],
               (r, c)).wait_recv()

    cot_copies = []
    for d in range(1, R):
        copy = remote(cots.at[r], cots.at[r], cot_send.at[d], cot_recv.at[r], (x_peers[d - 1], c))
        copy.start(priority=0)
        cot_copies.append(copy)
    for yy in y_peers:
        gather_send(c, col_of(z, yy, k))
    for zz in odd_peers[:H]:
        gather_send(c, col_of(zz, y, k))
    for i, zz in enumerate(even_peers):
        copy = remote(features, far_feat.at[zh], far_send.at[i], far_recv.at[zh], (r, col_of(zz, y, k)))
        copy.start(priority=0)
        pending_far.append(copy)
    gather_send(c, col_of(z, y, 1 - k))

    for load in loads[8:]:
        load.start(priority=1)
    with jax.named_scope("S07loads"):
        for copy in to_smem:
            copy.wait()
        for load in loads:
            load.wait()

    def add_slot(j, acc):
        acc = acc + tile_buf[code[0, j]].astype(F32)
        sums[j + 1] = acc
        return acc

    def pass_on(i):
        zz = z_peers[i]
        block = col_of(zz, y, k)
        if i < H:
            gather_wait(block)
        else:
            hh = lax.rem(zh + i - H + 1, H)
            remote(features, far_feat.at[hh], far_send.at[0], far_recv.at[hh], (r, c)).wait_recv()
            proj[block] = jnp.dot(far_feat[hh], weight[...], preferred_element_type=F32).astype(BF16)
            feat_t[i - H + 1] = far_feat[hh].astype(F32).T.astype(BF16)
        for yy in y_peers:
            gather_send(block, col_of(z, yy, k))
        if False and i == 0:
            for peer in even_peers:
                gather_send(block, col_of(peer, y, k))
        gather_send(block, col_of(z, y, 1 - k))

    parts = 8
    early = ()
    acc = jnp.zeros((side, side), F32)
    with jax.named_scope("S08sums"):
        for part in range(parts):
            acc = lax.fori_loop(part * slots // parts, (part + 1) * slots // parts, add_slot, acc,
                                unroll=8)
            for i, at in enumerate(early):
                if at == part and i < len(z_peers):
                    pass_on(i)

    with jax.named_scope("S09cot"):
        for d in range(1, R):
            peer = x_peers[d - 1]
            remote(cots.at[peer], cots.at[peer], cot_send.at[d], cot_recv.at[peer], (peer, c)).wait_recv()
            cots_t[peer] = cots[peer].astype(F32).T.astype(BF16)

    kept = dense.shape[0] == C

    def row_block(b, t, start):
        base = b * block_cells + t * per
        parts = []
        for e in range(per):
            end = sums[last[0, base + e + 1]]
            parts.append((end - start).astype(BF16))
            start = end
        return parts, start

    def back_block(b):
        at = b if kept else 0
        start = sums[last[0, b * block_cells]]
        for t in range(row_tiles):
            parts, start = row_block(b, t, start)
            for e in range(per):
                dense[at, t * side:(t + 1) * side, e * side:(e + 1) * side] = parts[e]
        left = jnp.concatenate([cots_t[s] for s in range(R)], axis=1)
        return jnp.dot(left, dense[at], preferred_element_type=F32)

    def z_order(i):
        late = i // H
        same = late * zl + (1 - late) * (1 - zl)
        return 2 * lax.rem(zh + 1 + lax.rem(i, H), H) + same

    def place(i):
        return z_order(lax.rem(i, O)), lax.rem(y + i // O + 1, I)

    def sib_copy(m):
        return remote(sib_out.at[m], sib_in.at[m], sib_send.at[m], sib_recv.at[m],
                      (r, col_of(z, y, 1 - k)))

    def send_sib(i, carry):
        zz, yy = place(i)
        m = zz * I + yy
        sib_out[m] = back_block(2 * m + 1 - k).astype(BF16)
        sib_copy(m).start()
        return carry

    def y_copy(zz, yy):
        return remote(y_out.at[zz * I + yy], y_in.at[y * O + zz], y_send.at[zz * I + yy],
                      y_recv.at[y * O + zz], (r, col_of(z, yy, k)))

    def send_y(i, carry):
        zz, yy = place(i)
        m = zz * I + yy
        mine = back_block(2 * m + k)
        sib_copy(m).wait_recv()
        y_out[m] = (mine + sib_in[m].astype(F32)).astype(BF16)
        y_copy(zz, yy).start()
        return carry

    with jax.named_scope("S10sib"):
        lax.fori_loop(0, O * (I - 1), send_sib, 0)
    with jax.named_scope("S11y"):
        lax.fori_loop(0, O * (I - 1), send_y, 0)
    with jax.named_scope("S12agfwda"):
        for i in range(len(early), 2):
            pass_on(i)
    with jax.named_scope("S12sib"):
        lax.fori_loop(O * (I - 1), O * I, send_sib, 0)
    with jax.named_scope("S12agfwdb"):
        for i in range(max(2, len(early)), 2):
            pass_on(i)

    def summed(zz):
        m = zz * I + y
        value = back_block(2 * m + k)
        sib_copy(m).wait_recv()
        value = value + sib_in[m].astype(F32)
        for yy in y_peers:
            slot = yy * O + zz
            remote(y_out.at[0], y_in.at[slot], y_send.at[0], y_recv.at[slot],
                   (r, c)).wait_recv()
            value = value + y_in[slot].astype(F32)
        return value

    z_copies = []
    with jax.named_scope("S13p"):
        for i in range(H):
            hh = lax.rem(zh + 1 + i, H)
            p_out[i] = summed(z_order(i)).astype(BF16)
            copy = remote(p_out.at[i], p_in.at[hh], p_send.at[i], p_recv.at[hh],
                          (r, col_of(partner, y, k)))
            copy.start()
            z_copies.append(copy)
    with jax.named_scope("S13late"):
        for i in range(2, O - 1):
            pass_on(i)
    term = jnp.zeros((feat_t.shape[1], proj.shape[2]), F32)
    z_late = []
    for i in range(H):
        with jax.named_scope("S14own"):
            hh = lax.rem(zh + 1 + i, H)
            value = summed(z_order(H + i))
        with jax.named_scope("S15pwait"):
            remote(p_out.at[0], p_in.at[hh], p_send.at[0], p_recv.at[hh], (r, c)).wait_recv()
            value = value + p_in[hh].astype(F32)
            if i < H - 1:
                z_out[i] = value.astype(BF16)
                copy = remote(z_out.at[i], z_in.at[zh], z_send.at[i], z_recv.at[zh],
                              (r, col_of(2 * hh + zl, y, k)))
                if False:
                    z_late.append(copy)
                else:
                    copy.start()
                z_copies.append(copy)
                term = term + jnp.dot(feat_t[i + 1], value.T.astype(BF16), preferred_element_type=F32)
    with jax.named_scope("S19term"):
        back_t = value
        term = term + jnp.dot(feat_t[0], value.T.astype(BF16), preferred_element_type=F32)
        term_out[...] = term.reshape(term_out.shape).astype(BF16)

    owners = term_out.shape[0]
    z_low, z_count = H - 1, 2
    group = z_count * I * 2

    def owner_device(o):
        kk = lax.rem(o, 2)
        yy = lax.rem(o // 2, I)
        zz = z_low + lax.rem(o // (2 * I), z_count)
        return o // group, col_of(zz, yy, kk)

    mine_o = ((r * z_count + z - z_low) * I + y) * 2 + k
    is_owner = (z >= z_low) & (z < z_low + z_count) & (mine_o < owners)

    def term_copy(o):
        return remote(term_out.at[o], term_in.at[me], term_send.at[0], term_recv.at[0],
                      owner_device(o))

    def bulk(count, send, recv):
        part = term_in.at[pl.ds(0, count)]
        return remote(part, part, send.at[0], recv.at[0], (r, c))

    def by_role(act):
        pl.when(is_owner)(lambda: act(owners - 1))
        pl.when(jnp.logical_not(is_owner))(lambda: act(owners))

    def tot_copy(t):
        return remote(total.at[mine_o], total.at[mine_o], tot_send.at[0], tot_recv.at[0],
                      (t // C, lax.rem(t, C)))

    with jax.named_scope("S20termsend"):
        @pl.when(is_owner)
        def _():
            def body(d, carry):
                term_copy(lax.rem(mine_o + d, owners)).start()
                return carry
            lax.fori_loop(1, owners, body, 0, unroll=owners - 1 if owners > 1 else 1)
            term_in[me] = term_out[mine_o]

        @pl.when(jnp.logical_not(is_owner))
        def _():
            def body(d, carry):
                term_copy(lax.rem(me + d, owners)).start()
                return carry
            lax.fori_loop(0, owners, body, 0, unroll=owners)

    for copy in z_late:
        copy.start()
    with jax.named_scope("S22agfwd"):
        for d in range(O):
            zz = lax.rem(z + d, O)
            for yy in y_peers:
                block = col_of(zz, yy, k)
                gather_wait(block)
                gather_send(block, col_of(z, y, 1 - k))
    with jax.named_scope("S23agwait"):
        for d in range(O):
            for e in range(I):
                gather_wait(col_of(lax.rem(z + d, O), lax.rem(y + e, I), 1 - k))

    wide = 4 if C % 4 == 0 else 1

    def forward(s):
        rows_of = pl.ds(pl.multiple_of(s * stretch, stretch), stretch)

        def stretch_block(b):
            if kept:
                return dense[b, rows_of, :]
            blocks = []
            for a in range(per):
                t = s * per + a
                parts, _ = row_block(b, t, sums[last[0, b * block_cells + t * per]])
                blocks.append(jnp.concatenate(parts, axis=1))
            return jnp.concatenate(blocks, axis=0)

        def step(g, out):
            left = jnp.concatenate([stretch_block(g * wide + b) for b in range(wide)], axis=1)
            right = jnp.concatenate([proj[g * wide + b] for b in range(wide)], axis=0)
            return out + jnp.dot(left, right, preferred_element_type=F32)
        return lax.fori_loop(0, C // wide, step, jnp.zeros((stretch, proj.shape[2]), F32))

    log_copies = []
    with jax.named_scope("S24fwdpeer"):
        for d in range(1, R):
            peer = x_peers[d - 1]
            log_out[d - 1] = forward(peer).astype(BF16)
            copy = remote(log_out.at[d - 1], log_in.at[r], log_send.at[d], log_recv.at[r], (peer, c))
            copy.start()
            log_copies.append(copy)

    with jax.named_scope("S25own"):
        @pl.when(is_owner)
        def _():
            bulk(n - 1, term_send, term_recv).wait_recv()
            whole = jnp.sum(term_in[...].astype(F32), axis=0) * (1.0 / math.sqrt(n * stretch))
            total[mine_o] = whole.astype(BF16)

            def body(d, carry):
                tot_copy(lax.rem(me + d, n)).start()
                return carry
            lax.fori_loop(1, n, body, 0, unroll=n - 1 if n <= 32 else 1)

    with jax.named_scope("S26fwdme"):
        mine_log = forward(r)
    with jax.named_scope("S27log"):
        for d in range(1, R):
            peer = x_peers[d - 1]
            remote(log_out.at[0], log_in.at[peer], log_send.at[0], log_recv.at[peer],
                   (peer, c)).wait_recv()
            mine_log = mine_log + log_in[peer].astype(F32)
        logits[...] = mine_log.astype(BF16)
    with jax.named_scope("S26gf"):
        for i in range(H - 1):
            hh = lax.rem(zh + 1 + i, H)
            remote(z_out.at[0], z_in.at[hh], z_send.at[0], z_recv.at[hh], (r, c)).wait_recv()
            back_t = back_t + z_in[hh].astype(F32)
        grad_features[...] = lax.dot_general(
            back_t.T.astype(BF16), weight[...], (((1,), (1,)), ((), ())),
            preferred_element_type=F32).astype(BF16)

    with jax.named_scope("S28drain"):
        for copy in pending + pending_far + cot_copies + log_copies + z_copies:
            copy.wait_send()

        def drain_sib(m, carry):
            sib_copy(m).wait_send()
            return carry

        lax.fori_loop(0, O * I, drain_sib, 0)

        def drain_y(i, carry):
            zz, yy = place(i)
            y_copy(zz, yy).wait_send()
            return carry

        lax.fori_loop(0, O * (I - 1), drain_y, 0)
        by_role(lambda count: bulk(count, term_send, term_recv).wait_send())
    with jax.named_scope("S29totwait"):
        by_role(lambda count: bulk(count, tot_send, tot_recv).wait_recv())
    with jax.named_scope("S30end"):
        grad_weight[...] = total[...].astype(F32).reshape(grad_weight.shape)

        @pl.when(is_owner)
        def _():
            bulk(n - 1, tot_send, tot_recv).wait_send()


def hand_over(a, b, c, x, y, z):
    x[...] = a[...]
    y[...] = b[...]
    z[...] = c[...]


def per_device(R, C, features, weight, tiles, slot_tile_row, tile_cols, live_tiles, cotangent):
    slots, side = tiles.shape[2], tiles.shape[3]
    stretch, width = features.shape
    out_width = weight.shape[1]
    half = C // 2
    O = 4 if half % 4 == 0 else 2
    H = O // 2
    I = half // O
    n = R * C
    per = stretch // side
    cells = R * per * C * per
    centre = R * 2 * I * 2
    owners = min(centre, width // 16)
    rows = width // owners
    chunks = 8 if slots % 8 == 0 else 1
    dma = pltpu.SemaphoreType.DMA
    vmem = pltpu.VMEM
    blk = (out_width, stretch)
    gathers = (O - 1) + (I - 1) + 1 + (O - 1) * I + O * (I - 1)
    scratch = [
        vmem((stretch, width), BF16),
        vmem((width, out_width), BF16),
        vmem((1, slots), jnp.int32),
        vmem((1, slots), jnp.int32),
        vmem((slots, side, side), BF16),
        vmem((slots + 1, side, side), F32),
        vmem((C if C * R <= 64 else 1, R * stretch, stretch), BF16),
        vmem((C, stretch, out_width), BF16),
        vmem((R, stretch, out_width), BF16),
        vmem((R,) + blk, BF16),
        vmem((H, width, stretch), BF16),
        vmem((1, slots), jnp.int32),
        vmem((1, cells + 128), jnp.int32),
        pltpu.SMEM((1, slots), jnp.int32),
        pltpu.SMEM((1, cells + 128), jnp.int32),
        vmem((half,) + blk, BF16),
        vmem((half,) + blk, BF16),
        vmem((half,) + blk, BF16),
        vmem((half,) + blk, BF16),
        vmem((H,) + blk, BF16),
        vmem((H,) + blk, BF16),
        vmem((H,) + blk, BF16),
        vmem((H,) + blk, BF16),
        vmem((max(R - 1, 1), stretch, out_width), BF16),
        vmem((R, stretch, out_width), BF16),
        vmem((H, stretch, width), BF16),
        vmem((owners, rows, out_width), BF16),
        vmem((n, rows, out_width), BF16),
        vmem((owners, rows, out_width), BF16),
        dma((chunks,)), dma((5,)), dma((2,)), dma((R,)), dma((R,)),
        dma((gathers,)), dma((C,)),
        dma((half,)), dma((half,)), dma((half,)), dma((half,)),
        dma((H,)), dma((H,)), dma((H,)), dma((H,)), dma((H,)), dma((H,)), dma((R,)), dma((R,)),
        dma((1,)), dma((1,)), dma((1,)), dma((1,)),
    ]
    v = pl.BlockSpec(memory_space=pltpu.VMEM)
    hbm = pl.BlockSpec(memory_space=pltpu.HBM)
    shapes = (
            jax.ShapeDtypeStruct((stretch, out_width), BF16),
            jax.ShapeDtypeStruct((stretch, width), BF16),
            jax.ShapeDtypeStruct((width, out_width), F32),
        )

    def in_hbm(x):
        return pltpu.with_memory_space_constraint(x, pltpu.HBM)

    results = pl.pallas_call(
        functools.partial(kernel, (R, C, O, I)),
        out_shape=tuple(vmem(s.shape, s.dtype) for s in shapes),
        in_specs=[hbm] * 5 + [pl.BlockSpec(memory_space=pltpu.SMEM), hbm],
        out_specs=(v, v, v),
        scratch_shapes=scratch,
        compiler_params=pltpu.CompilerParams(
            collective_id=0, has_side_effects=True, vmem_limit_bytes=52 * 1024 * 1024),
    )(in_hbm(features), in_hbm(weight), in_hbm(tiles.reshape(slots, side, side)),
      in_hbm(slot_tile_row.reshape(1, slots)), in_hbm(tile_cols.reshape(1, slots)), live_tiles,
      in_hbm(cotangent))
    results = [pltpu.with_memory_space_constraint(x, pltpu.VMEM) for x in results]
    return pl.pallas_call(hand_over, out_shape=shapes, in_specs=[v, v, v],
                          out_specs=(v, v, v))(*results)


def solution(mesh):
    R, C = mesh.shape["row"], mesh.shape["col"]
    placed = (
        P(("row", "col"), None),
        P(),
        P("row", "col", None, None, None),
        P("row", "col", None),
        P("row", "col", None),
        P("row", "col"),
        P(("row", "col"), None),
    )
    return jax.shard_map(
        functools.partial(per_device, R, C),
        mesh=mesh,
        in_specs=placed,
        out_specs=(P(("row", "col"), None), P(("row", "col"), None), P()),
        check_vma=False,
    )
```
